32 devices in a mesh: batch: 4 (over y, x), ctx: 8 (over z, core).
Axes of the slice: x: 2, y: 2, z: 4, core: 2. Of those that a mesh axis runs over, the one named last changes fastest.
Arguments:
- hidden: bfloat16 [4, 1024, 768], P('batch', 'ctx'), may hold values from -6 to 6
- cotangent: bfloat16 [4, 1024, 768], P('batch', 'ctx'), may hold values from -6 to 6
- w_qkv: bfloat16 [768, 2304], P(('batch', 'ctx')), may hold values from -3 to 3
- w_proj: bfloat16 [768, 768], P(('batch', 'ctx')), may hold values from -1.25 to 1.25
- w_inner: bfloat16 [768, 2304], P(('batch', 'ctx')), may hold values from -0.21875 to 0.21875
- w_down: bfloat16 [768, 1152], P(('batch', 'ctx')), may hold values from -0.1875 to 0.1875
- norm1_gain: bfloat16 [768], P(('batch', 'ctx')), may hold values from 0.5 to 1.5
- norm2_gain: bfloat16 [768], P(('batch', 'ctx')), may hold values from 0.5 to 1.5
Outputs:
- hidden_out: bfloat16 [4, 1024, 768], P('batch', 'ctx')
- hidden_grad: float32 [4, 1024, 768], P('batch', 'ctx')
- qkv_grad: float32 [768, 2304], P(('batch', 'ctx'))
- proj_grad: float32 [768, 768], P(('batch', 'ctx'))
- inner_grad: float32 [768, 2304], P(('batch', 'ctx'))
- down_grad: float32 [768, 1152], P(('batch', 'ctx'))
- norm1_grad: float32 [768], P(('batch', 'ctx'))
- norm2_grad: float32 [768], P(('batch', 'ctx'))
The draws below stay inside these ranges and needn't reach their ends.
All inputs are finite; a program needn't handle non-finite values.
Results may differ from the reference program's by a relative error of at most 0.02.
Values may be sent and summed in bfloat16 or wider, within the bound.
A program may use at most 192 MiB of HBM per device.

```python
import jax
import jax.numpy as jnp
from jax import lax

D = 768
HEADS = 12
HEAD_DIM = 64
FF = 1152
LEN = 1024
SEQS = 4


def draw_w_qkv(key, part):
    spread_scale = (D // 2) ** (-0.5)
    sample = jnp.clip(jax.random.normal(key, (D, 3 * D), jnp.float32), -6.0, 6.0)
    return (sample * spread_scale).astype(jnp.bfloat16)


def with_spikes(drawn, own_key, source, target, blocks, factor):
    def block_of(dim):
        return (jnp.arange(drawn.shape[dim]) // (drawn.shape[dim] // blocks)).reshape((-1,) + (1,) * (drawn.ndim - 1 - dim))

    one_side = jax.random.permutation(own_key, blocks)[block_of(target)]
    far = (block_of(target) + blocks // 2) % blocks
    return jnp.where((block_of(source) == one_side) | (block_of(source) == far), factor * drawn, drawn)


def level_of(stream_key, dims, shards, low, high):
    def one(dim, blocks):
        heights = jax.random.uniform(jax.random.fold_in(jax.random.fold_in(stream_key, 6), dim), (blocks,), jnp.float32, low / len(shards), high / len(shards))
        return jnp.repeat(jnp.exp(heights), dims[dim] // blocks).reshape((-1,) + (1,) * (len(dims) - dim - 1))

    loudness = one(*shards[0])
    for cut in shards[1:]:
        loudness = loudness * one(*cut)
    return loudness


def gaussian(own_key, shape, width, most, cuts=(), kind=jnp.bfloat16):
    drawn = width * jax.random.normal(own_key, shape, jnp.float32)
    if cuts:
        drawn = drawn * level_of(own_key, shape, cuts, -0.22, 0.18)
    return jnp.clip(drawn, -most, most).astype(kind)


def noise_with(key, shape, scale, most, pieces, heavy, kind=jnp.bfloat16):
    array = scale * jax.random.normal(key, shape, jnp.float32)
    if pieces:
        array = array * level_of(key, shape, pieces, -0.22, 0.18)
    return jnp.clip(with_spikes(array, jax.random.fold_in(key, 3), *heavy), -most, most).astype(kind)


def setup_inputs(seed: int = 0) -> dict:
    arg_keys = jax.random.split(jax.random.key(seed), 9)
    return {
        "hidden": gaussian(arg_keys[0], (SEQS, LEN, D), 1.0, 6.0, ((0, 4), (1, 8))),
        "cotangent": noise_with(arg_keys[1], (SEQS, LEN, D), 1.0, 6.0, ((0, 4), (1, 8)), (1, 2, 8, 2.0)),
        "w_qkv": draw_w_qkv(jax.random.fold_in(arg_keys[8], 71), 0),
        "w_proj": gaussian(arg_keys[3], (D, D), (D // 32) ** -0.5, 1.25, ((0, 32),)),
        "w_inner": gaussian(arg_keys[4], (D, 2 * FF), D ** -0.5, 0.21875, ((0, 32),)),
        "w_down": gaussian(arg_keys[5], (D, FF), FF ** -0.5, 0.1875, ((0, 32),)),
        "norm1_gain": jnp.clip(1.0 + 0.1 * jax.random.normal(arg_keys[6], (D,), jnp.float32), 0.5, 1.5).astype(jnp.bfloat16),
        "norm2_gain": jnp.clip(1.0 + 0.1 * jax.random.normal(arg_keys[7], (D,), jnp.float32), 0.5, 1.5).astype(jnp.bfloat16),
    }


norm_eps = 1e-05
rope_base = 160000.0

def apply_layer_norm(values, gain_vector):
    centre = lax.optimization_barrier(jnp.mean(values, axis=-1, keepdims=True))
    shifted = values - centre
    spread = lax.optimization_barrier(jnp.mean(shifted * shifted, axis=-1, keepdims=True))
    inverse = lax.rsqrt(spread + norm_eps)
    normed = shifted * inverse
    return (normed * gain_vector, normed, inverse)

def layer_norm_gradient(upstream, gain_vector, normed, inverse):
    scaled = upstream * gain_vector
    first_mean = lax.optimization_barrier(jnp.mean(scaled, axis=-1, keepdims=True))
    second_mean = lax.optimization_barrier(jnp.mean(scaled * normed, axis=-1, keepdims=True))
    return (inverse * (scaled - first_mean - normed * second_mean), lax.optimization_barrier(jnp.sum(upstream * normed, axis=0)))

def rope_tables(offset, row_count, head_width):
    half_dim = head_width // 2
    position = (offset + jnp.arange(row_count, dtype=jnp.int32)).astype(jnp.float32)
    exponent = jnp.arange(half_dim, dtype=jnp.int32).astype(jnp.float32) * (-2.0 / head_width)
    angles = position[:, None] * jnp.power(rope_base, exponent)[None, :]
    return (jnp.cos(angles), jnp.sin(angles))

def rotate(values, cosine, sine_table, direction):
    half_dim = values.shape[-1] // 2
    front_half = values[..., :half_dim]
    back_half = values[..., half_dim:]
    cos_rows = cosine[:, None, :]
    sin_rows = sine_table[:, None, :] * direction
    return jnp.concatenate([front_half * cos_rows - back_half * sin_rows, back_half * cos_rows + front_half * sin_rows], axis=-1)

def gelu_parts(act_input):
    normal_cdf = 0.5 * (1.0 + jax.scipy.special.erf(act_input * 0.7071067811865476))
    density = jnp.exp(-0.5 * act_input * act_input) * 0.3989422804014327
    return (act_input * normal_cdf, normal_cdf + act_input * density)

def rounded(values):
    return lax.optimization_barrier(values.astype(jnp.bfloat16)).astype(jnp.float32)

def reference(hidden, cotangent, w_qkv, w_proj, w_inner, w_down, norm1_gain, norm2_gain):
    seq_length = hidden.shape[1]
    block_rows = min(512, seq_length)
    block_count = seq_length // block_rows
    score_scale = HEAD_DIM ** (-0.5)
    highest = lax.Precision.HIGHEST
    first_norm_gain = norm1_gain.astype(jnp.float32)
    second_norm_gain = norm2_gain.astype(jnp.float32)
    cosine, sine_table = rope_tables(0, seq_length, HEAD_DIM)

    def one_sequence(grad_totals, sequence_pair):
        token_rows, upstream = sequence_pair
        input_tokens = token_rows.astype(jnp.float32)
        first_normed_rows, first_centered_rows, first_inverse_deviation = apply_layer_norm(input_tokens, first_norm_gain)
        h_one = first_normed_rows.astype(jnp.bfloat16)
        projected = jnp.dot(h_one, w_qkv, preferred_element_type=jnp.float32)
        query_rot = rotate(projected[:, :D].reshape(seq_length, HEADS, HEAD_DIM), cosine, sine_table, 1.0).astype(jnp.bfloat16)
        key_rot = rotate(projected[:, D:2 * D].reshape(seq_length, HEADS, HEAD_DIM), cosine, sine_table, 1.0).astype(jnp.bfloat16)
        value_rows = projected[:, 2 * D:].reshape(seq_length, HEADS, HEAD_DIM).astype(jnp.bfloat16)
        key_wide = key_rot.astype(jnp.float32)
        value_wide = value_rows.astype(jnp.float32)

        def attend(query_block):
            scores = jnp.einsum('qhd,khd->hqk', query_block.astype(jnp.float32), key_wide) * score_scale
            row_peak = lax.optimization_barrier(jnp.max(scores, axis=-1))
            log_total = row_peak + jnp.log(lax.optimization_barrier(jnp.sum(jnp.exp(scores - row_peak[..., None]), axis=-1)))
            weights_low = rounded(jnp.exp(scores - log_total[..., None]))
            mixture = jnp.einsum('hqk,khd->qhd', weights_low, value_wide, precision=highest)
            return (mixture, log_total)
        mixture, log_totals = lax.map(attend, query_rot.reshape(block_count, block_rows, HEADS, HEAD_DIM))
        attended = mixture.reshape(seq_length, D).astype(jnp.bfloat16)
        residual_stream = input_tokens + jnp.dot(attended, w_proj, preferred_element_type=jnp.float32)
        second_normed_rows, second_centered_rows, second_inverse_deviation = apply_layer_norm(residual_stream, second_norm_gain)
        h_two = second_normed_rows.astype(jnp.bfloat16)
        inner_all = jnp.dot(h_two, w_inner, preferred_element_type=jnp.float32)
        act_half = inner_all[:, :FF]
        gate_half = inner_all[:, FF:]
        activated, gelu_slope = gelu_parts(act_half)
        middle = (activated * gate_half).astype(jnp.bfloat16)
        output_rows = residual_stream + jnp.dot(middle, w_down.T, preferred_element_type=jnp.float32)
        d_middle = jnp.dot(upstream, w_down, preferred_element_type=jnp.float32)
        down_part = jnp.dot(upstream.T, middle, preferred_element_type=jnp.float32)
        d_inner = jnp.concatenate([d_middle * gate_half * gelu_slope, d_middle * activated], axis=-1).astype(jnp.bfloat16)
        inner_part = jnp.dot(h_two.T, d_inner, preferred_element_type=jnp.float32)
        second_hidden_gradient = jnp.dot(d_inner, w_inner.T, preferred_element_type=jnp.float32)
        residual_norm_gradient, second_gain_portion = layer_norm_gradient(second_hidden_gradient, second_norm_gain, second_centered_rows, second_inverse_deviation)
        d_resid = upstream.astype(jnp.float32) + residual_norm_gradient
        d_resid_low = d_resid.astype(jnp.bfloat16)
        proj_part = jnp.dot(attended.T, d_resid_low, preferred_element_type=jnp.float32)
        d_attended = jnp.dot(d_resid_low, w_proj.T, preferred_element_type=jnp.float32).astype(jnp.bfloat16)
        grad_heads = d_attended.reshape(seq_length, HEADS, HEAD_DIM)
        row_delta = lax.optimization_barrier(jnp.sum(grad_heads.astype(jnp.float32) * attended.reshape(seq_length, HEADS, HEAD_DIM).astype(jnp.float32), axis=-1))
        delta_blocks = jnp.transpose(row_delta.reshape(block_count, block_rows, HEADS), (0, 2, 1))

        def attend_back(running, block_items):
            query_block, grad_block, log_block, delta_block = block_items
            query_wide = query_block.astype(jnp.float32)
            grad_wide = grad_block.astype(jnp.float32)
            scores = jnp.einsum('qhd,khd->hqk', query_wide, key_wide) * score_scale
            probabilities = jnp.exp(scores - log_block[..., None])
            probs_low = rounded(probabilities)
            grad_dots = jnp.einsum('qhd,khd->hqk', grad_wide, value_wide)
            dscore = rounded(probabilities * (grad_dots - delta_block[..., None]))
            query_grad = jnp.einsum('hqk,khd->qhd', dscore, key_wide) * score_scale
            key_sum = running[0] + jnp.einsum('hqk,qhd->khd', dscore, query_wide) * score_scale
            value_sum = running[1] + jnp.einsum('hqk,qhd->khd', probs_low, grad_wide)
            return ((key_sum, value_sum), query_grad)
        zero_heads = jnp.zeros((seq_length, HEADS, HEAD_DIM), jnp.float32)
        (key_grad, value_grad), query_grad = lax.scan(attend_back, (zero_heads, zero_heads), (query_rot.reshape(block_count, block_rows, HEADS, HEAD_DIM), grad_heads.reshape(block_count, block_rows, HEADS, HEAD_DIM), log_totals, delta_blocks))
        query_grad = query_grad.reshape(seq_length, HEADS, HEAD_DIM)
        d_query = rotate(query_grad, cosine, sine_table, -1.0)
        d_key = rotate(key_grad, cosine, sine_table, -1.0)
        d_projected = jnp.concatenate([d_query.reshape(seq_length, D), d_key.reshape(seq_length, D), value_grad.reshape(seq_length, D)], axis=-1).astype(jnp.bfloat16)
        qkv_part = jnp.dot(h_one.T, d_projected, preferred_element_type=jnp.float32)
        first_hidden_gradient = jnp.dot(d_projected, w_qkv.T, preferred_element_type=jnp.float32)
        input_norm_gradient, first_gain_portion = layer_norm_gradient(first_hidden_gradient, first_norm_gain, first_centered_rows, first_inverse_deviation)
        input_grad = d_resid + input_norm_gradient
        new_totals = (grad_totals[0] + qkv_part, grad_totals[1] + proj_part, grad_totals[2] + inner_part, grad_totals[3] + down_part, grad_totals[4] + first_gain_portion, grad_totals[5] + second_gain_portion)
        return (new_totals, (output_rows.astype(jnp.bfloat16), input_grad))
    start_totals = (jnp.zeros((D, 3 * D), jnp.float32), jnp.zeros((D, D), jnp.float32), jnp.zeros((D, 2 * FF), jnp.float32), jnp.zeros((D, FF), jnp.float32), jnp.zeros((D,), jnp.float32), jnp.zeros((D,), jnp.float32))
    grad_totals, (hidden_out, hidden_grad) = lax.scan(one_sequence, start_totals, (hidden, cotangent))
    return (hidden_out, hidden_grad, grad_totals[0], grad_totals[1], grad_totals[2], grad_totals[3], grad_totals[4], grad_totals[5])
```

```python
import functools
import math

import jax
import jax.numpy as jnp
from jax import lax
from jax.experimental import pallas as pl
from jax.experimental.pallas import tpu as pltpu
from jax.sharding import PartitionSpec as P

D = 768
HEADS = 12
HEAD_DIM = 64
FF = 1152


norm_eps = 1e-05
rope_base = 160000.0


def apply_layer_norm(values, gain_vector):
    centre = jnp.mean(values, axis=-1, keepdims=True)
    shifted = values - centre
    spread = jnp.mean(shifted * shifted, axis=-1, keepdims=True)
    inverse = lax.rsqrt(spread + norm_eps)
    normed = shifted * inverse
    return (normed * gain_vector, normed, inverse)


def layer_norm_gradient(upstream, gain_vector, normed, inverse):
    scaled = upstream * gain_vector
    first_mean = jnp.mean(scaled, axis=-1, keepdims=True)
    second_mean = jnp.mean(scaled * normed, axis=-1, keepdims=True)
    return (
        inverse * (scaled - first_mean - normed * second_mean),
        jnp.sum(upstream * normed, axis=0),
    )


def rope_tables(offset, row_count, head_width):
    half_dim = head_width // 2
    position = (offset + jnp.arange(row_count, dtype=jnp.int32)).astype(jnp.float32)
    exponent = jnp.arange(half_dim, dtype=jnp.int32).astype(jnp.float32) * (-2.0 / head_width)
    angles = position[:, None] * jnp.power(rope_base, exponent)[None, :]
    return (jnp.cos(angles), jnp.sin(angles))


def rotate(values, cosine, sine_table, direction):
    half_dim = values.shape[-1] // 2
    front_half = values[..., :half_dim]
    back_half = values[..., half_dim:]
    cos_rows = cosine[:, None, :]
    sin_rows = sine_table[:, None, :] * direction
    return jnp.concatenate(
        [
            front_half * cos_rows - back_half * sin_rows,
            back_half * cos_rows + front_half * sin_rows,
        ],
        axis=-1,
    )


def gelu_parts(act_input):
    normal_cdf = 0.5 * (1.0 + jax.scipy.special.erf(act_input * 0.7071067811865476))
    density = jnp.exp(-0.5 * act_input * act_input) * 0.3989422804014327
    return (act_input * normal_cdf, normal_cdf + act_input * density)


def as_heads(flat_rows):
    return flat_rows.reshape(flat_rows.shape[0], HEADS, HEAD_DIM)


EVERY = ("batch", "ctx")
LANES = 128


def weight_grad_kernel(bounds, *refs):
    count = len(bounds) - 1
    lefts, rights, gains_ref, out_ref = refs[:count], refs[count : 2 * count], refs[-2], refs[-1]
    step = pl.program_id(0)
    for index in range(count):

        @pl.when(jnp.logical_and(step >= bounds[index], step < bounds[index + 1]))
        def _(left=lefts[index], right=rights[index]):
            out_ref[...] = lax.dot_general(
                left[...],
                right[...],
                (((0,), (0,)), ((), ())),
                preferred_element_type=jnp.float32,
            ).astype(out_ref.dtype)

    @pl.when(step == bounds[count])
    def _():
        out_ref[:, :LANES] = gains_ref[...].astype(out_ref.dtype)


def weight_grads(pairs, gain_columns):
    rows, width = pairs[0][0].shape
    widths = [right.shape[1] for _, right in pairs]
    block = math.gcd(*widths)
    bounds = [0]
    for part in widths:
        bounds.append(bounds[-1] + part // block)

    def right_index(start, count, step):
        return (0, jnp.clip(step - start, 0, count - 1))

    whole = lambda step: (0, 0)
    total = sum(widths) + LANES
    return pl.pallas_call(
        functools.partial(weight_grad_kernel, tuple(bounds)),
        out_shape=jax.ShapeDtypeStruct((width, total), jnp.bfloat16),
        grid=(bounds[-1] + 1,),
        in_specs=[pl.BlockSpec((rows, width), whole) for _ in pairs]
        + [
            pl.BlockSpec(
                (rows, block),
                functools.partial(right_index, bounds[i], bounds[i + 1] - bounds[i]),
            )
            for i in range(len(pairs))
        ]
        + [pl.BlockSpec((width, LANES), whole)],
        out_specs=pl.BlockSpec((width, block), lambda step: (0, step)),
        cost_estimate=pl.CostEstimate(
            flops=2 * rows * width * total, bytes_accessed=2 * width * total, transcendentals=0
        ),
    )(*[left for left, _ in pairs], *[right for _, right in pairs], gain_columns)


def local(hidden, cotangent, w_qkv, w_proj, w_inner, w_down, norm1_gain, norm2_gain):
    token_rows = hidden.shape[1]
    score_scale = HEAD_DIM ** (-0.5)
    gains = jnp.pad(jnp.stack([norm1_gain, norm2_gain], axis=1), ((0, 0), (0, LANES - 2)))
    packed = lax.all_gather(
        jnp.concatenate([w_qkv, w_proj, w_inner, w_down, gains], axis=1), EVERY, axis=0, tiled=True
    )
    edges = [0]
    for part in (w_qkv, w_proj, w_inner, w_down, gains):
        edges.append(edges[-1] + part.shape[1])
    full_qkv, full_proj, full_inner, full_down, full_gains = (
        packed[:, edges[i] : edges[i + 1]] for i in range(5)
    )
    first_norm_gain = full_gains[:, 0].astype(jnp.float32)
    second_norm_gain = full_gains[:, 1].astype(jnp.float32)
    input_tokens = hidden[0].astype(jnp.float32)
    first_normed_rows, first_centered_rows, first_inverse_deviation = apply_layer_norm(
        input_tokens, first_norm_gain
    )
    h_one = first_normed_rows.astype(jnp.bfloat16)
    projected = jnp.dot(h_one, full_qkv, preferred_element_type=jnp.float32)
    cosine, sine_table = rope_tables(lax.axis_index("ctx") * token_rows, token_rows, HEAD_DIM)
    query_rot = rotate(as_heads(projected[:, :D]), cosine, sine_table, 1.0).astype(jnp.bfloat16)
    key_flat = (
        rotate(as_heads(projected[:, D : 2 * D]), cosine, sine_table, 1.0)
        .astype(jnp.bfloat16)
        .reshape(token_rows, D)
    )
    value_flat = projected[:, 2 * D :].astype(jnp.bfloat16)
    key_value = lax.all_gather(
        jnp.concatenate([key_flat, value_flat], axis=1), "ctx", axis=0, tiled=True
    )
    key_whole = as_heads(key_value[:, :D])
    value_whole = as_heads(key_value[:, D:])
    scores = (
        jnp.einsum("qhd,khd->hqk", query_rot, key_whole, preferred_element_type=jnp.float32)
        * score_scale
    )
    row_peak = jnp.max(scores, axis=-1)
    weights = jnp.exp(scores - row_peak[..., None])
    row_total = jnp.sum(weights, axis=-1)
    mixture = jnp.einsum(
        "hqk,khd->qhd",
        weights.astype(jnp.bfloat16),
        value_whole,
        preferred_element_type=jnp.float32,
    )
    attended = (
        (mixture / jnp.transpose(row_total)[:, :, None])
        .reshape(token_rows, D)
        .astype(jnp.bfloat16)
    )
    residual_stream = input_tokens + jnp.dot(
        attended, full_proj, preferred_element_type=jnp.float32
    )
    second_normed_rows, second_centered_rows, second_inverse_deviation = apply_layer_norm(
        residual_stream, second_norm_gain
    )
    h_two = second_normed_rows.astype(jnp.bfloat16)
    inner_all = jnp.dot(h_two, full_inner, preferred_element_type=jnp.float32)
    act_half = inner_all[:, :FF]
    gate_half = inner_all[:, FF:]
    activated, gelu_slope = gelu_parts(act_half)
    middle = (activated * gate_half).astype(jnp.bfloat16)
    output_rows = residual_stream + jnp.einsum(
        "tf,df->td", middle, full_down, preferred_element_type=jnp.float32
    )
    upstream = cotangent[0]
    d_middle = jnp.dot(upstream, full_down, preferred_element_type=jnp.float32)
    d_inner = jnp.concatenate(
        [d_middle * gate_half * gelu_slope, d_middle * activated], axis=-1
    ).astype(jnp.bfloat16)
    second_hidden_gradient = jnp.einsum(
        "te,de->td", d_inner, full_inner, preferred_element_type=jnp.float32
    )
    residual_norm_gradient, second_gain_portion = layer_norm_gradient(
        second_hidden_gradient, second_norm_gain, second_centered_rows, second_inverse_deviation
    )
    d_resid = upstream.astype(jnp.float32) + residual_norm_gradient
    d_resid_low = d_resid.astype(jnp.bfloat16)
    d_attended = jnp.einsum(
        "td,ed->te", d_resid_low, full_proj, preferred_element_type=jnp.float32
    ).astype(jnp.bfloat16)
    grad_heads = as_heads(d_attended)
    row_delta = jnp.transpose(
        jnp.sum(grad_heads.astype(jnp.float32) * as_heads(attended).astype(jnp.float32), axis=-1)
    )
    probabilities = weights * (1.0 / row_total)[..., None]
    grad_dots = jnp.einsum(
        "qhd,khd->hqk", grad_heads, value_whole, preferred_element_type=jnp.float32
    )
    dscore = (probabilities * (grad_dots - row_delta[..., None])).astype(jnp.bfloat16)
    probs_low = probabilities.astype(jnp.bfloat16)
    key_terms = (
        jnp.einsum("hqk,qhd->khd", dscore, query_rot, preferred_element_type=jnp.float32)
        * score_scale
    )
    value_terms = jnp.einsum(
        "hqk,qhd->khd", probs_low, grad_heads, preferred_element_type=jnp.float32
    )
    whole_rows = key_value.shape[0]
    key_value_sum = lax.psum_scatter(
        jnp.concatenate(
            [
                key_terms.reshape(whole_rows, D).astype(jnp.bfloat16),
                value_terms.reshape(whole_rows, D).astype(jnp.bfloat16),
            ],
            axis=1,
        ),
        "ctx",
        scatter_dimension=0,
        tiled=True,
    )
    query_grad = (
        jnp.einsum("hqk,khd->qhd", dscore, key_whole, preferred_element_type=jnp.float32)
        * score_scale
    )
    d_query = rotate(query_grad, cosine, sine_table, -1.0)
    d_key = rotate(as_heads(key_value_sum[:, :D].astype(jnp.float32)), cosine, sine_table, -1.0)
    d_projected = jnp.concatenate(
        [
            d_query.reshape(token_rows, D).astype(jnp.bfloat16),
            d_key.reshape(token_rows, D).astype(jnp.bfloat16),
            key_value_sum[:, D:],
        ],
        axis=-1,
    )
    first_hidden_gradient = jnp.einsum(
        "te,de->td", d_projected, full_qkv, preferred_element_type=jnp.float32
    )
    input_norm_gradient, first_gain_portion = layer_norm_gradient(
        first_hidden_gradient, first_norm_gain, first_centered_rows, first_inverse_deviation
    )
    input_grad = d_resid + input_norm_gradient
    gain_columns = jnp.pad(
        jnp.stack([first_gain_portion, second_gain_portion], axis=1), ((0, 0), (0, LANES - 2))
    )
    grad_terms = weight_grads(
        [(h_one, d_projected), (attended, d_resid_low), (h_two, d_inner), (upstream, middle)],
        gain_columns,
    )
    grad_share = lax.psum_scatter(
        grad_terms, EVERY, scatter_dimension=0, tiled=True
    ).astype(jnp.float32)
    return (
        output_rows.astype(jnp.bfloat16)[None],
        input_grad[None],
        grad_share[:, edges[0] : edges[1]],
        grad_share[:, edges[1] : edges[2]],
        grad_share[:, edges[2] : edges[3]],
        grad_share[:, edges[3] : edges[4]],
        grad_share[:, edges[4]],
        grad_share[:, edges[4] + 1],
    )


def solution(mesh):
    placed = (
        P("batch", "ctx", None),
        P("batch", "ctx", None),
        P(("batch", "ctx"), None),
        P(("batch", "ctx"), None),
        P(("batch", "ctx"), None),
        P(("batch", "ctx"), None),
        P(("batch", "ctx")),
        P(("batch", "ctx")),
    )
    return jax.shard_map(
        local,
        mesh=mesh,
        in_specs=placed,
        out_specs=(
            P("batch", "ctx", None),
            P("batch", "ctx", None),
            P(("batch", "ctx"), None),
            P(("batch", "ctx"), None),
            P(("batch", "ctx"), None),
            P(("batch", "ctx"), None),
            P(("batch", "ctx")),
            P(("batch", "ctx")),
        ),
        check_vma=False,
    )
```
